512 devices in a mesh: row: 32 (over z, y_hi, core), col: 16 (over y_lo, x).
Axes of the slice: x: 4, y: 8 (y_hi: 2, y_lo: 4; y = y_hi * 4 + y_lo), z: 8, core: 2. Of those that a mesh axis runs over, the one named last changes fastest.
Arguments:
- left_blocks: bfloat16 [32, 16, 4, 256, 256], P('row', 'col'), may hold values from -6 to 6
- left_rows: int32 [32, 16, 4], P('row', 'col'), may hold values from 0 to 15, as said below
- left_cols: int32 [32, 16, 4], P('row', 'col'), may hold values from 0 to 31, as said below
- left_count: int32 [32, 16], P('row', 'col'), may hold values from 1 to 4, as said below
- right_blocks: bfloat16 [32, 16, 1, 256, 256], P('row', 'col'), may hold values from -0.375 to 0.375
- right_rows: int32 [32, 16, 1], P('row', 'col'), may hold values from 0 to 15, as said below
- right_cols: int32 [32, 16, 1], P('row', 'col'), may hold values from 0 to 31, as said below
- kept_rows: int32 [32, 2], P('row'), may hold values from 0 to 15, as said below
- kept_cols: int32 [16, 4], P('col'), may hold values from 0 to 31, as said below
Outputs:
- product: bfloat16 [32, 16, 2, 4, 256, 256], P('row', 'col')
The draws below stay inside these ranges and needn't reach their ends.
Inputs may be any that keep to these rules, and one draw needn't show every extreme that they name: `left_rows`: each entry is one of the 2 entries of kept_rows for its row panel. For a slot of contraction panel k, left_cols = u * 16 + v with u 0 or 1, where v is one of the block rows that right_rows lists for sub-panel 2 * k + u (the same on every column panel). `left_count`: slots at or past the count are unused and hold arbitrary blocks and indices; some panel uses all 4 slots. `right_rows`: all column panels of one sub-panel list the same 1 distinct block rows. `right_cols`: each entry is one of the 4 entries of kept_cols for its column panel. `kept_rows`: distinct within a row panel. `kept_cols`: distinct within a column panel.
All inputs are finite; a program needn't handle non-finite values.
Results may differ from the reference program's by a relative error of at most 0.001.
Values may be sent and summed in bfloat16 or wider, within the bound.
No kernel may reach another device: no remote copies, remote signals or barrier semaphores. Data moves between devices by JAX's collectives and lax.ppermute only.
A program may use at most 64 MiB of HBM per device.

```python
import jax
import jax.numpy as jnp
from jax import lax

BS = 256
RB = 16
SA = 4
SB = 1
RA = 2
CA = 4
CB = 32
ROW_PANELS = 32
COL_PANELS = 16


def layout(key):
    streams = jax.random.split(jax.random.fold_in(key, 7), 8)
    kept_rows = jax.vmap(lambda single: jax.random.permutation(single, RB)[:RA])(jax.random.split(streams[0], ROW_PANELS)).astype(jnp.int32)
    kept_cols = jax.vmap(lambda single: jax.random.permutation(single, CB)[:CA])(jax.random.split(streams[1], COL_PANELS)).astype(jnp.int32)
    active = jax.vmap(lambda single: jax.random.permutation(single, RB)[:SB])(jax.random.split(streams[2], ROW_PANELS)).astype(jnp.int32)
    right_rows = jnp.broadcast_to(active[:, None, :], (ROW_PANELS, COL_PANELS, SB))
    pick_col = jax.random.randint(streams[3], (ROW_PANELS, COL_PANELS, SB), 0, CA)
    right_cols = jnp.take_along_axis(jnp.broadcast_to(kept_cols[None, :, :], (ROW_PANELS, COL_PANELS, CA)), pick_col, axis=2).astype(jnp.int32)
    pick_row = jax.random.randint(streams[4], (ROW_PANELS, COL_PANELS, SA), 0, RA)
    left_rows = jnp.take_along_axis(jnp.broadcast_to(kept_rows[:, None, :], (ROW_PANELS, COL_PANELS, RA)), pick_row, axis=2).astype(jnp.int32)
    half_pick = jax.random.randint(streams[5], (ROW_PANELS, COL_PANELS, SA), 0, 2)
    slot_pick = jax.random.randint(streams[6], (ROW_PANELS, COL_PANELS, SA), 0, SB)
    panel_ids = jnp.arange(COL_PANELS, dtype=jnp.int32)[None, :, None]
    sub_panel = 2 * panel_ids + half_pick
    left_cols = (half_pick * RB + active.reshape(-1)[sub_panel * SB + slot_pick]).astype(jnp.int32)
    left_count = jax.random.randint(streams[7], (ROW_PANELS, COL_PANELS), 1, SA + 1).at[0, 0].set(SA).astype(jnp.int32)
    return (left_rows, left_cols, left_count, right_rows, right_cols, kept_rows, kept_cols)


def draw_left_rows(key, part):
    return layout(key)[0]


def draw_left_cols(key, part):
    return layout(key)[1]


def draw_left_count(key, part):
    return layout(key)[2]


def draw_right_rows(key, part):
    return layout(key)[3]


def draw_right_cols(key, part):
    return layout(key)[4]


def draw_kept_rows(key, part):
    return layout(key)[5]


def draw_kept_cols(key, part):
    return layout(key)[6]


def steps_of(rng, extent, cuts, least, top_value):
    gain = 1.0
    for axis_at, shards_of in cuts:
        draws = jax.random.uniform(jax.random.fold_in(jax.random.fold_in(rng, 6), axis_at), (shards_of,), jnp.float32, least / len(cuts), top_value / len(cuts))
        gain = gain * jnp.repeat(jnp.exp(draws), extent[axis_at] // shards_of).reshape((-1,) + (1,) * (len(extent) - 1 - axis_at))
    return gain


def noise(stream_key, extent, scale, reach, pieces=(), kind=jnp.bfloat16):
    drawn = jax.random.normal(stream_key, extent, jnp.float32) * scale
    if len(pieces) > 0:
        drawn = steps_of(stream_key, extent, pieces, -0.22, 0.18) * drawn
    return jnp.clip(drawn, min=-reach, max=reach).astype(kind)


def setup_inputs(seed: int = 0) -> dict:
    arg_keys = jax.random.split(jax.random.key(seed), 10)
    left_blocks = noise(arg_keys[0], (ROW_PANELS, COL_PANELS, SA, BS, BS), 1.0, 6.0, ((0, 32), (1, 16)))
    left_rows = draw_left_rows(jax.random.fold_in(arg_keys[9], 71), 0)
    left_cols = draw_left_cols(jax.random.fold_in(arg_keys[9], 71), 0)
    left_count = draw_left_count(jax.random.fold_in(arg_keys[9], 71), 0)
    right_blocks = noise(arg_keys[4], (ROW_PANELS, COL_PANELS, SB, BS, BS), BS ** -0.5, 0.375, ((0, 32), (1, 16)))
    right_rows = draw_right_rows(jax.random.fold_in(arg_keys[9], 71), 0)
    right_cols = draw_right_cols(jax.random.fold_in(arg_keys[9], 71), 0)
    kept_rows = draw_kept_rows(jax.random.fold_in(arg_keys[9], 71), 0)
    kept_cols = draw_kept_cols(jax.random.fold_in(arg_keys[9], 71), 0)
    return {"left_blocks": left_blocks, "left_rows": left_rows, "left_cols": left_cols, "left_count": left_count, "right_blocks": right_blocks, "right_rows": right_rows, "right_cols": right_cols, "kept_rows": kept_rows, "kept_cols": kept_cols}


def device_block(flat_index, left_blocks, left_rows, left_cols, left_count, right_blocks, right_rows, right_cols, kept_rows, kept_cols):
    row_panel = flat_index // COL_PANELS
    col_panel = flat_index % COL_PANELS
    halves = ROW_PANELS // COL_PANELS
    left_panel = left_blocks[row_panel].astype(jnp.float32)
    right_panel = right_blocks[:, col_panel].astype(jnp.float32).reshape(COL_PANELS, halves, SB, BS, BS)
    offsets = (RB * jnp.arange(halves)).astype(jnp.int32)
    right_contract = right_rows[:, col_panel].reshape(COL_PANELS, halves, SB) + offsets[None, :, None]
    right_column = right_cols[:, col_panel].reshape(COL_PANELS, halves, SB)
    live_slot = jnp.arange(SA).astype(jnp.int32)[None, :] < left_count[row_panel][:, None]
    matched = (left_cols[row_panel][:, :, None, None] == right_contract[:, None, :, :]) & live_slot[:, :, None, None]
    row_hit = left_rows[row_panel][:, :, None] == kept_rows[row_panel][None, None, :]
    col_hit = right_column[:, :, :, None] == kept_cols[col_panel][None, None, None, :]
    weights = (matched[:, :, :, :, None, None] & row_hit[:, :, None, None, :, None] & col_hit[:, None, :, :, None, :]).astype(jnp.float32)
    products = jnp.einsum("kamn,kubnp->kaubmp", left_panel, right_panel, precision=lax.Precision.HIGHEST)
    summed = jnp.einsum("kaubij,kaubmp->ijmp", weights, products, precision=lax.Precision.HIGHEST)
    return summed.astype(jnp.bfloat16)


def reference(left_blocks, left_rows, left_cols, left_count, right_blocks, right_rows, right_cols, kept_rows, kept_cols):
    indices = jnp.arange(ROW_PANELS * COL_PANELS).astype(jnp.int32)
    stacked = lax.map(lambda flat_index: device_block(flat_index, left_blocks, left_rows, left_cols, left_count, right_blocks, right_rows, right_cols, kept_rows, kept_cols), indices)
    return stacked.reshape(ROW_PANELS, COL_PANELS, RA, CA, BS, BS)
```

```python
import jax
import jax.numpy as jnp
from jax import lax
from jax.experimental import pallas as pl
from jax.experimental.pallas import tpu as pltpu
from jax.sharding import Mesh
from jax.sharding import PartitionSpec as P

RB = 16
BS = 256
META = 16
ROW = ("z", "h", "c")
COL = ("y", "x")
SWAP = [(0, 1), (1, 0)]
ROUND_Z = [(2 * z, 2 * ((z + 1) % 8)) for z in range(8)] + [(2 * z + 1, 2 * ((z - 1) % 8) + 1) for z in range(8)]


def meta_rows(columns):
    count, width = columns.shape
    padded = jnp.zeros((META, BS), jnp.int32).at[:count, :width].set(columns)
    return padded.astype(jnp.bfloat16)


def product_kernel(left_meta, right_meta, *refs):
    right_refs = refs[:-5]
    left_ref, out_ref, acc_ref, right_all, where_ref = refs[-5:]
    step = pl.program_id(0)

    @pl.when(step == 0)
    def _():
        acc_ref[...] = jnp.zeros_like(acc_ref)
        slot = 0
        for ref in right_refs:
            for place in range(ref.shape[0]):
                right_all[slot] = ref[place, :BS, :]
                where_ref[right_meta[slot, 0]] = slot
                slot += 1

    for a in range(4):
        code = left_meta[step * 4 + a, 0]
        at = where_ref[jnp.maximum(code, 0) // 2]
        live = (code >= 0) & (left_meta[step * 4 + a, 1] == right_meta[at, 2])

        @pl.when(live)
        def _():
            block = (code % 2) * 4 + right_meta[at, 1]
            acc_ref[block] += jnp.dot(
                left_ref[0, a * BS : (a + 1) * BS, :], right_all[at], preferred_element_type=jnp.float32
            )

    @pl.when(step == pl.num_programs(0) - 1)
    def _():
        out_ref[...] = acc_ref[...].astype(jnp.bfloat16)


def product(left, left_meta, rights, right_meta):
    whole = [pl.BlockSpec(r.shape, lambda k, lm, rm: (0, 0, 0)) for r in rights]
    return pl.pallas_call(
        product_kernel,
        grid_spec=pltpu.PrefetchScalarGridSpec(
            num_scalar_prefetch=2,
            grid=(left.shape[0],),
            in_specs=whole + [pl.BlockSpec((1,) + left.shape[1:], lambda k, lm, rm: (k, 0, 0))],
            out_specs=pl.BlockSpec((8, BS, BS), lambda k, lm, rm: (0, 0, 0)),
            scratch_shapes=[
                pltpu.VMEM((8, BS, BS), jnp.float32),
                pltpu.VMEM((32, BS, BS), jnp.bfloat16),
                pltpu.SMEM((32,), jnp.int32),
            ],
        ),
        out_shape=jax.ShapeDtypeStruct((8, BS, BS), jnp.bfloat16),
    )(left_meta, right_meta, *rights, left)


def place_in(values, kept):
    hit = values[:, None] == kept[None, :]
    return jnp.sum(jnp.where(hit, jnp.arange(kept.shape[0], dtype=jnp.int32)[None, :], 0), axis=1)


def body(
    left_blocks,
    left_rows,
    left_cols,
    left_count,
    right_blocks,
    right_rows,
    right_cols,
    kept_rows,
    kept_cols,
):
    panel_k = lax.axis_index(COL)
    own_q = lax.axis_index(ROW)
    cols = left_cols[0, 0]
    live = jnp.arange(4, dtype=jnp.int32) < left_count[0, 0]
    code = (2 * panel_k + cols // RB) * 2 + place_in(left_rows[0, 0], kept_rows[0])
    left_own = jnp.concatenate(
        [
            left_blocks[0, 0].reshape(4 * BS, BS),
            meta_rows(jnp.stack([jnp.where(live, code, -1), cols % RB], axis=1)),
        ]
    )
    right_own = jnp.concatenate(
        [
            right_blocks[0, 0, 0],
            meta_rows(jnp.stack([own_q[None], place_in(right_cols[0, 0], kept_cols[0]), right_rows[0, 0]], axis=1)),
        ]
    )
    lefts = lax.all_gather(left_own, COL)

    across = lax.ppermute(right_own, "h", SWAP)
    pair = jnp.stack([right_own, across])
    four = jnp.concatenate([pair, lax.ppermute(pair, "c", SWAP)])
    rounds = [four]
    for _ in range(3):
        rounds.append(lax.ppermute(rounds[-1], ("z", "c"), ROUND_Z))
    rounds.append(lax.ppermute(rounds[-1][:2], ("z", "c"), ROUND_Z))
    rights = rounds + [lax.ppermute(r, "c", SWAP) for r in rounds[1:]]
    right_meta = jnp.concatenate([r[:, BS, :3] for r in rights]).astype(jnp.int32)
    left_meta = lefts[:, 4 * BS : 4 * BS + 4, :2].reshape(64, 2).astype(jnp.int32)
    total = product(lefts, left_meta, rights, right_meta)
    return total.reshape(1, 1, 2, 4, BS, BS)


def solution(mesh):
    split = Mesh(mesh.devices.reshape(8, 2, 2, 4, 4), ROW + COL)
    return jax.shard_map(
        body,
        mesh=split,
        in_specs=(
            P(ROW, COL, None, None, None),
            P(ROW, COL, None),
            P(ROW, COL, None),
            P(ROW, COL),
            P(ROW, COL, None, None, None),
            P(ROW, COL, None),
            P(ROW, COL, None),
            P(ROW, None),
            P(COL, None),
        ),
        out_specs=P(ROW, COL, None, None, None, None),
        check_vma=False,
    )
```

```python
import jax
import jax.numpy as jnp
from jax import lax
from jax.experimental import pallas as pl
from jax.experimental.pallas import tpu as pltpu
from jax.sharding import Mesh
from jax.sharding import PartitionSpec as P

RB = 16
BS = 256
META = 16
HALF = 2 * BS + META
RIGHT = BS + META
DEAD = 8
GRANT = 4 << 20
ROW = ("z", "h", "c")
COL = ("y", "x")
SWAP = [(0, 1), (1, 0)]
ROUND_Z = [(2 * z, 2 * ((z + 1) % 8)) for z in range(8)] + [(2 * z + 1, 2 * ((z - 1) % 8) + 1) for z in range(8)]


VMEM = pl.BlockSpec(memory_space=pltpu.VMEM)
SMEM = pl.BlockSpec(memory_space=pltpu.SMEM)


def near(arrays):
    return [pltpu.with_memory_space_constraint(x, pltpu.VMEM) for x in arrays]


def turn(shift):
    return [(i, (i + shift) % 4) for i in range(4)]


def mirror(bit):
    return [(i, i ^ bit) for i in range(4)]


def write_meta(panel, values):
    lane = lax.broadcasted_iota(jnp.int32, (META, BS), 1)
    row = jnp.zeros((META, BS), jnp.int32)
    for place, value in enumerate(values):
        row = jnp.where(lane == place, value, row)
    panel[...] = row.astype(jnp.float32).astype(jnp.bfloat16)


def position(value, kept):
    place = jnp.int32(0)
    for n in range(1, kept.shape[1]):
        place = jnp.where(value == kept[0, n], n, place)
    return place


def prepare_kernel(*refs):
    blocks, right = refs[:2]
    count, right_row, right_col = refs[6:9]
    left_out, right_out = refs[9:11]
    rows, cols, kept_rows, kept_cols = refs[11:15]
    sems = refs[15]
    pairs = list(zip(refs[2:6], refs[11:15]))
    pairs += [(blocks.at[half], left_out.at[half, : 2 * BS]) for half in range(2)]
    pairs.append((right, right_out.at[:BS]))
    copies = [pltpu.make_async_copy(source, target, sems.at[n]) for n, (source, target) in enumerate(pairs)]
    for copy in copies:
        copy.start()
    panel_k = lax.axis_index("y") * 4 + lax.axis_index("x")
    own_q = lax.axis_index("z") * 4 + lax.axis_index("h") * 2 + lax.axis_index("c")
    for copy in copies[:4]:
        copy.wait()
    for half in range(2):
        values = []
        for slot in (2 * half, 2 * half + 1):
            col = cols[0, slot]
            code = (2 * panel_k + col // RB) * 2 + position(rows[0, slot], kept_rows)
            values += [jnp.where(slot < count[0, 0], code, -1), col % RB]
        write_meta(left_out.at[half, 2 * BS :], values)
    write_meta(right_out.at[BS:], [own_q, position(right_col[0, 0], kept_cols), right_row[0, 0]])
    for copy in copies[4:]:
        copy.wait()


def prepare(arrays, scalars):
    return pl.pallas_call(
        prepare_kernel,
        in_specs=[pl.BlockSpec(memory_space=pltpu.HBM)] * len(arrays) + [SMEM] * len(scalars),
        out_specs=(VMEM, VMEM),
        out_shape=(pltpu.VMEM((2, HALF, BS), jnp.bfloat16), pltpu.VMEM((RIGHT, BS), jnp.bfloat16)),
        scratch_shapes=[pltpu.SMEM(x.shape, jnp.int32) for x in arrays[2:]] + [pltpu.SemaphoreType.DMA((7,))],
        compiler_params=pltpu.CompilerParams(vmem_limit_bytes=GRANT),
    )(*[pltpu.with_memory_space_constraint(x, pltpu.HBM) for x in arrays], *scalars)


def read_meta(ref, count, first, tab, row):
    for place in range(count):
        tab[row + place, :] = ref[place, first : first + META, :128].astype(jnp.float32).astype(jnp.int32)[0]


def add_slots(left_refs, table, row, right_ref, right_tab, acc_ref):
    for ref in left_refs:

        def one_half(half, carry, ref=ref, row=row):
            for a in range(2):
                code = table[row + half, 2 * a]
                q = jnp.maximum(code, 0) // 2
                live = (code >= 0) & (table[row + half, 2 * a + 1] == right_tab[1, q])
                block = jnp.where(live, (code % 2) * 4 + right_tab[0, q], DEAD)
                acc_ref[block] += jnp.dot(
                    ref[half, a * BS : (a + 1) * BS, :], right_ref[q], preferred_element_type=jnp.float32
                )

            return carry

        lax.fori_loop(0, ref.shape[0], one_half, 0)
        row += ref.shape[0]


def first_kernel(rights, *refs):
    right_refs, left_refs = refs[:rights], refs[rights:-6]
    acc_ref, right_all, right_tab, tab, table, sem = refs[-6:]
    row = 0
    for ref in right_refs:
        read_meta(ref, ref.shape[0], BS, tab, row)
        row += ref.shape[0]
    for ref in left_refs:
        read_meta(ref, ref.shape[0], 2 * BS, tab, row)
        row += ref.shape[0]
    copy = pltpu.make_async_copy(tab, table, sem)
    copy.start()
    acc_ref[...] = jnp.zeros_like(acc_ref)
    copy.wait()
    row = 0
    for ref in right_refs:
        for place in range(ref.shape[0]):
            q = table[row, 0]
            right_all[q] = ref[place, :BS, :]
            right_tab[0, q] = table[row, 1]
            right_tab[1, q] = table[row, 2]
            row += 1
    add_slots(left_refs, table, row, right_all, right_tab, acc_ref)


def last_kernel(acc_ref, right_all, right_tab, *refs):
    left_refs = refs[:-5]
    _, out_ref, tab, table, sem = refs[-5:]
    row = 0
    for ref in left_refs:
        read_meta(ref, ref.shape[0], 2 * BS, tab, row)
        row += ref.shape[0]
    copy = pltpu.make_async_copy(tab, table, sem)
    copy.start()
    copy.wait()
    add_slots(left_refs, table, 0, right_all, right_tab, acc_ref)
    out_ref[...] = acc_ref[:8].astype(jnp.bfloat16)


def table_scratch(panels):
    count = -(-sum(x.shape[0] for x in panels) // 8) * 8
    return [pltpu.VMEM((count, 128), jnp.int32), pltpu.SMEM((count, 128), jnp.int32), pltpu.SemaphoreType.DMA]


def first_product(lefts, rights):
    return pl.pallas_call(
        lambda *refs: first_kernel(len(rights), *refs),
        in_specs=[VMEM] * (len(lefts) + len(rights)),
        out_specs=(VMEM, VMEM, SMEM),
        out_shape=(
            pltpu.VMEM((9, BS, BS), jnp.float32),
            pltpu.VMEM((32, BS, BS), jnp.bfloat16),
            jax.ShapeDtypeStruct((2, 32), jnp.int32),
        ),
        scratch_shapes=table_scratch(rights + lefts),
        compiler_params=pltpu.CompilerParams(vmem_limit_bytes=GRANT),
    )(*near(rights + lefts))


def last_product(lefts, total, right_all, right_tab):
    return pl.pallas_call(
        last_kernel,
        in_specs=[VMEM, VMEM, SMEM] + [VMEM] * len(lefts),
        out_specs=(VMEM, VMEM),
        out_shape=(pltpu.VMEM((9, BS, BS), jnp.float32), jax.ShapeDtypeStruct((8, BS, BS), jnp.bfloat16)),
        input_output_aliases={0: 0},
        scratch_shapes=table_scratch(lefts),
        compiler_params=pltpu.CompilerParams(vmem_limit_bytes=GRANT),
    )(*near([total, right_all]), right_tab, *near(lefts))[1]


def panels(
    left_blocks,
    left_rows,
    left_cols,
    left_count,
    right_blocks,
    right_rows,
    right_cols,
    kept_rows,
    kept_cols,
):
    left_own, right_own = prepare(
        [
            left_blocks.reshape(2, 2 * BS, BS),
            right_blocks.reshape(BS, BS),
            left_rows.reshape(1, 4),
            left_cols.reshape(1, 4),
            kept_rows,
            kept_cols,
        ],
        [left_count, right_rows.reshape(1, 1), right_cols.reshape(1, 1)],
    )

    groups = [left_own] + [lax.ppermute(left_own, "y", mirror(bit)) for bit in (1, 2, 3)]
    arrived = []
    for place, panel in enumerate(groups):
        up = lax.ppermute(panel, "x", turn(1))
        down = lax.ppermute(panel, "x", turn(-1))
        if place < 3:
            far = [lax.ppermute(up[:1], "x", turn(1)), lax.ppermute(down[1:], "x", turn(-1))]
        else:
            far = [lax.ppermute(panel, "x", turn(2))]
        arrived.append([panel, up, down] + far)

    pair = jnp.stack([right_own, lax.ppermute(right_own, "h", SWAP)])
    four = jnp.concatenate([pair, lax.ppermute(pair, "c", SWAP)])
    rounds = [four]
    for place in (1, 2, 3, 4):
        rounds.append(lax.ppermute(rounds[-1] if place < 4 else rounds[-1][:2], ("z", "c"), ROUND_Z))
    passed = jnp.concatenate(rounds[1:])
    rights = [four, passed, lax.ppermute(passed, "c", SWAP)]

    carried = first_product(sum(arrived[:3], []), rights)
    return last_product(arrived[3], *carried).reshape(1, 1, 2, 4, BS, BS)


def solution(mesh):
    split = Mesh(mesh.devices.reshape(8, 2, 2, 4, 4), ROW + COL)
    return jax.shard_map(
        panels,
        mesh=split,
        in_specs=(
            P(ROW, COL, None, None, None),
            P(ROW, COL, None),
            P(ROW, COL, None),
            P(ROW, COL),
            P(ROW, COL, None, None, None),
            P(ROW, COL, None),
            P(ROW, COL, None),
            P(ROW, None),
            P(COL, None),
        ),
        out_specs=P(ROW, COL, None, None, None, None),
        check_vma=False,
    )
```

```python
import jax
import jax.numpy as jnp
from jax import lax
from jax.experimental import pallas as pl
from jax.experimental.pallas import tpu as pltpu
from jax.sharding import Mesh
from jax.sharding import PartitionSpec as P

RB = 16
BS = 256
META = 16
HALF = 2 * BS + META
RIGHT = BS + META
DEAD = 8
GRANT = 4 << 20
ROW = ("z", "h", "c")
COL = ("y", "x")
SWAP = [(0, 1), (1, 0)]
ROUND_Z = [(2 * z, 2 * ((z + 1) % 8)) for z in range(8)] + [(2 * z + 1, 2 * ((z - 1) % 8) + 1) for z in range(8)]


VMEM = pl.BlockSpec(memory_space=pltpu.VMEM)
SMEM = pl.BlockSpec(memory_space=pltpu.SMEM)


def near(arrays):
    return [pltpu.with_memory_space_constraint(x, pltpu.VMEM) for x in arrays]


def turn(shift):
    return [(i, (i + shift) % 4) for i in range(4)]


def mirror(bit):
    return [(i, i ^ bit) for i in range(4)]


def write_meta(panel, values):
    lane = lax.broadcasted_iota(jnp.int32, (META, BS), 1)
    row = jnp.zeros((META, BS), jnp.int32)
    for place, value in enumerate(values):
        row = jnp.where(lane == place, value, row)
    panel[...] = row.astype(jnp.float32).astype(jnp.bfloat16)


def position(value, kept):
    place = jnp.int32(0)
    for n in range(1, kept.shape[1]):
        place = jnp.where(value == kept[0, n], n, place)
    return place


def prepare_kernel(*refs):
    blocks, right = refs[:2]
    count, right_row, right_col = refs[6:9]
    left_out, right_out = refs[9:11]
    rows, cols, kept_rows, kept_cols = refs[11:15]
    sems = refs[15]
    pairs = list(zip(refs[2:6], refs[11:15]))
    pairs += [(blocks.at[half], left_out.at[half, : 2 * BS]) for half in range(2)]
    pairs.append((right, right_out.at[:BS]))
    copies = [pltpu.make_async_copy(source, target, sems.at[n]) for n, (source, target) in enumerate(pairs)]
    for copy in copies:
        copy.start()
    panel_k = lax.axis_index("y") * 4 + lax.axis_index("x")
    own_q = lax.axis_index("z") * 4 + lax.axis_index("h") * 2 + lax.axis_index("c")
    for copy in copies[:4]:
        copy.wait()
    for half in range(2):
        values = []
        for slot in (2 * half, 2 * half + 1):
            col = cols[0, slot]
            code = (2 * panel_k + col // RB) * 2 + position(rows[0, slot], kept_rows)
            values += [jnp.where(slot < count[0, 0], code, -1), col % RB]
        write_meta(left_out.at[half, 2 * BS :], values)
    write_meta(right_out.at[BS:], [own_q, position(right_col[0, 0], kept_cols), right_row[0, 0]])
    for copy in copies[4:]:
        copy.wait()


def prepare(arrays, scalars):
    return pl.pallas_call(
        prepare_kernel,
        in_specs=[pl.BlockSpec(memory_space=pltpu.HBM)] * len(arrays) + [SMEM] * len(scalars),
        out_specs=(VMEM, VMEM),
        out_shape=(pltpu.VMEM((2, HALF, BS), jnp.bfloat16), pltpu.VMEM((RIGHT, BS), jnp.bfloat16)),
        scratch_shapes=[pltpu.SMEM(x.shape, jnp.int32) for x in arrays[2:]] + [pltpu.SemaphoreType.DMA((7,))],
        compiler_params=pltpu.CompilerParams(vmem_limit_bytes=GRANT),
    )(*[pltpu.with_memory_space_constraint(x, pltpu.HBM) for x in arrays], *scalars)


def read_meta(ref, count, first, tab, row):
    for place in range(count):
        tab[row + place, :] = ref[place, first : first + META, :128].astype(jnp.float32).astype(jnp.int32)[0]


def add_slots(left_refs, table, row, right_ref, right_tab, acc_ref):
    for ref in left_refs:

        def one_half(half, carry, ref=ref, row=row):
            for a in range(2):
                code = table[row + half, 2 * a]
                q = jnp.maximum(code, 0) // 2
                live = (code >= 0) & (table[row + half, 2 * a + 1] == right_tab[1, q])
                block = jnp.where(live, (code % 2) * 4 + right_tab[0, q], DEAD)
                acc_ref[block] += jnp.dot(
                    ref[half, a * BS : (a + 1) * BS, :], right_ref[q], preferred_element_type=jnp.float32
                )

            return carry

        lax.fori_loop(0, ref.shape[0], one_half, 0)
        row += ref.shape[0]


def first_kernel(rights, *refs):
    right_refs, left_refs = refs[:rights], refs[rights:-6]
    acc_ref, right_all, right_tab, tab, table, sem = refs[-6:]
    row = 0
    for ref in right_refs:
        read_meta(ref, ref.shape[0], BS, tab, row)
        row += ref.shape[0]
    for ref in left_refs:
        read_meta(ref, ref.shape[0], 2 * BS, tab, row)
        row += ref.shape[0]
    copy = pltpu.make_async_copy(tab, table, sem)
    copy.start()
    acc_ref[...] = jnp.zeros_like(acc_ref)
    copy.wait()
    row = 0
    for ref in right_refs:
        for place in range(ref.shape[0]):
            q = table[row, 0]
            right_all[q] = ref[place, :BS, :]
            right_tab[0, q] = table[row, 1]
            right_tab[1, q] = table[row, 2]
            row += 1
    add_slots(left_refs, table, row, right_all, right_tab, acc_ref)


def last_kernel(acc_ref, right_all, right_tab, *refs):
    left_refs = refs[:-5]
    _, out_ref, tab, table, sem = refs[-5:]
    row = 0
    for ref in left_refs:
        read_meta(ref, ref.shape[0], 2 * BS, tab, row)
        row += ref.shape[0]
    copy = pltpu.make_async_copy(tab, table, sem)
    copy.start()
    copy.wait()
    add_slots(left_refs, table, 0, right_all, right_tab, acc_ref)
    out_ref[...] = acc_ref[:8].astype(jnp.bfloat16)


def table_scratch(panels):
    count = -(-sum(x.shape[0] for x in panels) // 8) * 8
    return [pltpu.VMEM((count, 128), jnp.int32), pltpu.SMEM((count, 128), jnp.int32), pltpu.SemaphoreType.DMA]


def first_product(lefts, rights):
    return pl.pallas_call(
        lambda *refs: first_kernel(len(rights), *refs),
        in_specs=[VMEM] * (len(lefts) + len(rights)),
        out_specs=(VMEM, VMEM, SMEM),
        out_shape=(
            pltpu.VMEM((9, BS, BS), jnp.float32),
            pltpu.VMEM((32, BS, BS), jnp.bfloat16),
            jax.ShapeDtypeStruct((2, 32), jnp.int32),
        ),
        scratch_shapes=table_scratch(rights + lefts),
        compiler_params=pltpu.CompilerParams(vmem_limit_bytes=GRANT),
    )(*near(rights + lefts))


def last_product(lefts, total, right_all, right_tab):
    return pl.pallas_call(
        last_kernel,
        in_specs=[VMEM, VMEM, SMEM] + [VMEM] * len(lefts),
        out_specs=(VMEM, VMEM),
        out_shape=(pltpu.VMEM((9, BS, BS), jnp.float32), jax.ShapeDtypeStruct((8, BS, BS), jnp.bfloat16)),
        input_output_aliases={0: 0},
        scratch_shapes=table_scratch(lefts),
        compiler_params=pltpu.CompilerParams(vmem_limit_bytes=GRANT),
    )(*near([total, right_all]), right_tab, *near(lefts))[1]


def panels(
    left_blocks,
    left_rows,
    left_cols,
    left_count,
    right_blocks,
    right_rows,
    right_cols,
    kept_rows,
    kept_cols,
):
    left_own, right_own = prepare(
        [
            left_blocks.reshape(2, 2 * BS, BS),
            right_blocks.reshape(BS, BS),
            left_rows.reshape(1, 4),
            left_cols.reshape(1, 4),
            kept_rows,
            kept_cols,
        ],
        [left_count, right_rows.reshape(1, 1), right_cols.reshape(1, 1)],
    )

    beside = lax.ppermute(left_own, "y", mirror(1))
    across = lax.ppermute(left_own, "y", mirror(2))
    groups = [left_own, beside, across, lax.ppermute(across, "y", mirror(1))]
    far = lax.ppermute(groups[3], "x", turn(2))
    arrived = list(groups)
    up, down = groups[0], groups[0]
    for place in range(4):
        if place:
            up = jnp.concatenate([groups[place], up[:1]])
            down = jnp.concatenate([groups[place], down[1:2]])
        up = lax.ppermute(up, "x", turn(1))
        down = lax.ppermute(down, "x", turn(-1))
        arrived += [up, down]

    pair = jnp.stack([right_own, lax.ppermute(right_own, "h", SWAP)])
    four = jnp.concatenate([pair, lax.ppermute(pair, "c", SWAP)])
    rounds = [four]
    for place in (1, 2, 3, 4):
        rounds.append(lax.ppermute(rounds[-1] if place < 4 else rounds[-1][:2], ("z", "c"), ROUND_Z))
    passed = jnp.concatenate(rounds[1:])
    rights = [four, passed, lax.ppermute(passed, "c", SWAP)]

    carried = first_product(arrived[:-2], rights)
    return last_product(arrived[-2:] + [far], *carried).reshape(1, 1, 2, 4, BS, BS)


def solution(mesh):
    split = Mesh(mesh.devices.reshape(8, 2, 2, 4, 4), ROW + COL)
    return jax.shard_map(
        panels,
        mesh=split,
        in_specs=(
            P(ROW, COL, None, None, None),
            P(ROW, COL, None),
            P(ROW, COL, None),
            P(ROW, COL),
            P(ROW, COL, None, None, None),
            P(ROW, COL, None),
            P(ROW, COL, None),
            P(ROW, None),
            P(COL, None),
        ),
        out_specs=P(ROW, COL, None, None, None, None),
        check_vma=False,
    )
```

```python
import jax
import jax.numpy as jnp
from jax import lax
from jax.experimental import pallas as pl
from jax.experimental.pallas import tpu as pltpu
from jax.sharding import Mesh
from jax.sharding import PartitionSpec as P

RB = 16
BS = 256
META = 16
HALF = 2 * BS + META
RIGHT = BS + META
DEAD = 8
GRANT = 4 << 20
ROW = ("z", "h", "c")
COL = ("y", "x")
SWAP = [(0, 1), (1, 0)]
ROUND_Z = [(2 * z, 2 * ((z + 1) % 8)) for z in range(8)] + [(2 * z + 1, 2 * ((z - 1) % 8) + 1) for z in range(8)]


EVEN = [(0, 1), (1, 0), (2, 3), (3, 2)]
ODD = [(1, 2), (2, 1), (3, 0), (0, 3)]


VMEM = pl.BlockSpec(memory_space=pltpu.VMEM)
SMEM = pl.BlockSpec(memory_space=pltpu.SMEM)


def near(arrays):
    return [pltpu.with_memory_space_constraint(x, pltpu.VMEM) for x in arrays]


def mirror(bit):
    return [(i, i ^ bit) for i in range(4)]


def write_meta(panel, values):
    lane = lax.broadcasted_iota(jnp.int32, (META, BS), 1)
    row = jnp.zeros((META, BS), jnp.int32)
    for place, value in enumerate(values):
        row = jnp.where(lane == place, value, row)
    panel[...] = row.astype(jnp.float32).astype(jnp.bfloat16)


def position(value, kept):
    place = jnp.int32(0)
    for n in range(1, kept.shape[1]):
        place = jnp.where(value == kept[0, n], n, place)
    return place


def prepare_kernel(*refs):
    blocks, right = refs[:2]
    count, right_row, right_col = refs[6:9]
    left_out, right_out = refs[9:11]
    rows, cols, kept_rows, kept_cols = refs[11:15]
    sems = refs[15]
    pairs = list(zip(refs[2:6], refs[11:15]))
    pairs += [(blocks.at[half], left_out.at[half, : 2 * BS]) for half in range(2)]
    pairs.append((right, right_out.at[:BS]))
    copies = [pltpu.make_async_copy(source, target, sems.at[n]) for n, (source, target) in enumerate(pairs)]
    for copy in copies:
        copy.start()
    panel_k = lax.axis_index("y") * 4 + lax.axis_index("x")
    own_q = lax.axis_index("z") * 4 + lax.axis_index("h") * 2 + lax.axis_index("c")
    for copy in copies[:4]:
        copy.wait()
    for half in range(2):
        values = []
        for slot in (2 * half, 2 * half + 1):
            col = cols[0, slot]
            code = (2 * panel_k + col // RB) * 2 + position(rows[0, slot], kept_rows)
            values += [jnp.where(slot < count[0, 0], code, -1), col % RB]
        write_meta(left_out.at[half, 2 * BS :], values)
    write_meta(right_out.at[BS:], [own_q, position(right_col[0, 0], kept_cols), right_row[0, 0]])
    for copy in copies[4:]:
        copy.wait()


def prepare(arrays, scalars):
    return pl.pallas_call(
        prepare_kernel,
        in_specs=[pl.BlockSpec(memory_space=pltpu.HBM)] * len(arrays) + [SMEM] * len(scalars),
        out_specs=(VMEM, VMEM),
        out_shape=(pltpu.VMEM((2, HALF, BS), jnp.bfloat16), pltpu.VMEM((RIGHT, BS), jnp.bfloat16)),
        scratch_shapes=[pltpu.SMEM(x.shape, jnp.int32) for x in arrays[2:]] + [pltpu.SemaphoreType.DMA((7,))],
        compiler_params=pltpu.CompilerParams(vmem_limit_bytes=GRANT),
    )(*[pltpu.with_memory_space_constraint(x, pltpu.HBM) for x in arrays], *scalars)


def read_meta(ref, count, first, tab, row):
    for place in range(count):
        tab[row + place, :] = ref[place, first : first + META, :128].astype(jnp.float32).astype(jnp.int32)[0]


def add_slots(left_refs, table, row, right_ref, right_tab, acc_ref):
    for ref in left_refs:

        def one_half(half, carry, ref=ref, row=row):
            for a in range(2):
                code = table[row + half, 2 * a]
                q = jnp.maximum(code, 0) // 2
                live = (code >= 0) & (table[row + half, 2 * a + 1] == right_tab[1, q])
                block = jnp.where(live, (code % 2) * 4 + right_tab[0, q], DEAD)
                acc_ref[block] += jnp.dot(
                    ref[half, a * BS : (a + 1) * BS, :], right_ref[q], preferred_element_type=jnp.float32
                )

            return carry

        lax.fori_loop(0, ref.shape[0], one_half, 0)
        row += ref.shape[0]


def first_kernel(rights, *refs):
    right_refs, left_refs = refs[:rights], refs[rights:-6]
    acc_ref, right_all, right_tab, tab, table, sem = refs[-6:]
    row = 0
    for ref in right_refs:
        read_meta(ref, ref.shape[0], BS, tab, row)
        row += ref.shape[0]
    for ref in left_refs:
        read_meta(ref, ref.shape[0], 2 * BS, tab, row)
        row += ref.shape[0]
    copy = pltpu.make_async_copy(tab, table, sem)
    copy.start()
    acc_ref[...] = jnp.zeros_like(acc_ref)
    copy.wait()
    row = 0
    for ref in right_refs:
        for place in range(ref.shape[0]):
            q = table[row, 0]
            right_all[q] = ref[place, :BS, :]
            right_tab[0, q] = table[row, 1]
            right_tab[1, q] = table[row, 2]
            row += 1
    add_slots(left_refs, table, row, right_all, right_tab, acc_ref)


def last_kernel(acc_ref, right_all, right_tab, *refs):
    left_refs = refs[:-5]
    _, out_ref, tab, table, sem = refs[-5:]
    row = 0
    for ref in left_refs:
        read_meta(ref, ref.shape[0], 2 * BS, tab, row)
        row += ref.shape[0]
    copy = pltpu.make_async_copy(tab, table, sem)
    copy.start()
    copy.wait()
    add_slots(left_refs, table, 0, right_all, right_tab, acc_ref)
    out_ref[...] = acc_ref[:8].astype(jnp.bfloat16)


def table_scratch(panels):
    count = -(-sum(x.shape[0] for x in panels) // 8) * 8
    return [pltpu.VMEM((count, 128), jnp.int32), pltpu.SMEM((count, 128), jnp.int32), pltpu.SemaphoreType.DMA]


def first_product(lefts, rights):
    return pl.pallas_call(
        lambda *refs: first_kernel(len(rights), *refs),
        in_specs=[VMEM] * (len(lefts) + len(rights)),
        out_specs=(VMEM, VMEM, SMEM),
        out_shape=(
            pltpu.VMEM((9, BS, BS), jnp.float32),
            pltpu.VMEM((32, BS, BS), jnp.bfloat16),
            jax.ShapeDtypeStruct((2, 32), jnp.int32),
        ),
        scratch_shapes=table_scratch(rights + lefts),
        compiler_params=pltpu.CompilerParams(vmem_limit_bytes=GRANT),
    )(*near(rights + lefts))


def last_product(lefts, total, right_all, right_tab):
    return pl.pallas_call(
        last_kernel,
        in_specs=[VMEM, VMEM, SMEM] + [VMEM] * len(lefts),
        out_specs=(VMEM, VMEM),
        out_shape=(pltpu.VMEM((9, BS, BS), jnp.float32), jax.ShapeDtypeStruct((8, BS, BS), jnp.bfloat16)),
        input_output_aliases={0: 0},
        scratch_shapes=table_scratch(lefts),
        compiler_params=pltpu.CompilerParams(vmem_limit_bytes=GRANT),
    )(*near([total, right_all]), right_tab, *near(lefts))[1]


def panels(
    left_blocks,
    left_rows,
    left_cols,
    left_count,
    right_blocks,
    right_rows,
    right_cols,
    kept_rows,
    kept_cols,
):
    left_own, right_own = prepare(
        [
            left_blocks.reshape(2, 2 * BS, BS),
            right_blocks.reshape(BS, BS),
            left_rows.reshape(1, 4),
            left_cols.reshape(1, 4),
            kept_rows,
            kept_cols,
        ],
        [left_count, right_rows.reshape(1, 1), right_cols.reshape(1, 1)],
    )

    far = lax.ppermute(left_own, "x", mirror(2))
    across = lax.ppermute(left_own, "y", mirror(2))
    beside = lax.ppermute(left_own, "y", mirror(1))
    diagonal = lax.ppermute(across, "y", mirror(1))
    far_across = lax.ppermute(far, "y", mirror(2))
    far_beside = lax.ppermute(far, "y", mirror(1))
    far_diagonal = lax.ppermute(far_across, "y", mirror(1))
    early = [left_own, far, across, beside, diagonal, far_across, far_beside]
    late = [far_diagonal]
    for place, panel in enumerate([left_own, jnp.concatenate([beside, across]), diagonal]):
        got = [lax.ppermute(panel, "x", EVEN), lax.ppermute(panel, "x", ODD)]
        if place < 2:
            early += got
        else:
            late += got

    pair = jnp.stack([right_own, lax.ppermute(right_own, "h", SWAP)])
    four = jnp.concatenate([pair, lax.ppermute(pair, "c", SWAP)])
    rounds = [four]
    for place in (1, 2, 3, 4):
        rounds.append(lax.ppermute(rounds[-1] if place < 4 else rounds[-1][:2], ("z", "c"), ROUND_Z))
    passed = jnp.concatenate(rounds[1:])
    rights = [four, passed, lax.ppermute(passed, "c", SWAP)]

    carried = first_product(early, rights)
    return last_product(late, *carried).reshape(1, 1, 2, 4, BS, BS)


def solution(mesh):
    split = Mesh(mesh.devices.reshape(8, 2, 2, 4, 4), ROW + COL)
    return jax.shard_map(
        panels,
        mesh=split,
        in_specs=(
            P(ROW, COL, None, None, None),
            P(ROW, COL, None),
            P(ROW, COL, None),
            P(ROW, COL),
            P(ROW, COL, None, None, None),
            P(ROW, COL, None),
            P(ROW, COL, None),
            P(ROW, None),
            P(COL, None),
        ),
        out_specs=P(ROW, COL, None, None, None, None),
        check_vma=False,
    )
```

```python
import jax
import jax.numpy as jnp
from jax import lax
from jax.experimental import pallas as pl
from jax.experimental.pallas import tpu as pltpu
from jax.sharding import Mesh
from jax.sharding import PartitionSpec as P

RB = 16
BS = 256
META = 16
HALF = 2 * BS + META
RIGHT = BS + META
DEAD = 8
GRANT = 4 << 20
ROW = ("z", "h", "c")
COL = ("y", "x")
SWAP = [(0, 1), (1, 0)]


EVEN = [(0, 1), (1, 0), (2, 3), (3, 2)]
ODD = [(1, 2), (2, 1), (3, 0), (0, 3)]


VMEM = pl.BlockSpec(memory_space=pltpu.VMEM)
SMEM = pl.BlockSpec(memory_space=pltpu.SMEM)


def near(arrays):
    return [pltpu.with_memory_space_constraint(x, pltpu.VMEM) for x in arrays]


def along_z(step):
    up = [(2 * z, 2 * ((z + step) % 8)) for z in range(8)]
    return up + [(2 * z + 1, 2 * ((z - step) % 8) + 1) for z in range(8)]


def mirror(bit):
    return [(i, i ^ bit) for i in range(4)]


def write_meta(panel, values):
    lane = lax.broadcasted_iota(jnp.int32, (META, BS), 1)
    row = jnp.zeros((META, BS), jnp.int32)
    for place, value in enumerate(values):
        row = jnp.where(lane == place, value, row)
    panel[...] = row.astype(jnp.float32).astype(jnp.bfloat16)


def position(value, kept):
    place = jnp.int32(0)
    for n in range(1, kept.shape[1]):
        place = jnp.where(value == kept[0, n], n, place)
    return place


def prepare_kernel(*refs):
    blocks, right = refs[:2]
    count, right_row, right_col = refs[6:9]
    left_out, right_out = refs[9:11]
    rows, cols, kept_rows, kept_cols = refs[11:15]
    sems = refs[15]
    pairs = list(zip(refs[2:6], refs[11:15]))
    pairs += [(blocks.at[half], left_out.at[half, : 2 * BS]) for half in range(2)]
    pairs.append((right, right_out.at[:BS]))
    copies = [pltpu.make_async_copy(source, target, sems.at[n]) for n, (source, target) in enumerate(pairs)]
    for copy in copies:
        copy.start()
    panel_k = lax.axis_index("y") * 4 + lax.axis_index("x")
    own_q = lax.axis_index("z") * 4 + lax.axis_index("h") * 2 + lax.axis_index("c")
    for copy in copies[:4]:
        copy.wait()
    for half in range(2):
        values = []
        for slot in (2 * half, 2 * half + 1):
            col = cols[0, slot]
            code = (2 * panel_k + col // RB) * 2 + position(rows[0, slot], kept_rows)
            values += [jnp.where(slot < count[0, 0], code, -1), col % RB]
        write_meta(left_out.at[half, 2 * BS :], values)
    write_meta(right_out.at[BS:], [own_q, position(right_col[0, 0], kept_cols), right_row[0, 0]])
    for copy in copies[4:]:
        copy.wait()


def prepare(arrays, scalars):
    return pl.pallas_call(
        prepare_kernel,
        in_specs=[pl.BlockSpec(memory_space=pltpu.HBM)] * len(arrays) + [SMEM] * len(scalars),
        out_specs=(VMEM, VMEM),
        out_shape=(pltpu.VMEM((2, HALF, BS), jnp.bfloat16), pltpu.VMEM((RIGHT, BS), jnp.bfloat16)),
        scratch_shapes=[pltpu.SMEM(x.shape, jnp.int32) for x in arrays[2:]] + [pltpu.SemaphoreType.DMA((7,))],
        compiler_params=pltpu.CompilerParams(vmem_limit_bytes=GRANT),
    )(*[pltpu.with_memory_space_constraint(x, pltpu.HBM) for x in arrays], *scalars)


def read_meta(ref, count, first, tab, row):
    for place in range(count):
        tab[row + place, :] = ref[place, first : first + META, :128].astype(jnp.float32).astype(jnp.int32)[0]


def add_slots(left_refs, table, row, right_ref, right_tab, acc_ref):
    for ref in left_refs:

        def one_half(half, carry, ref=ref, row=row):
            for a in range(2):
                code = table[row + half, 2 * a]
                q = jnp.maximum(code, 0) // 2
                live = (code >= 0) & (table[row + half, 2 * a + 1] == right_tab[1, q])
                block = jnp.where(live, (code % 2) * 4 + right_tab[0, q], DEAD)
                acc_ref[block] += jnp.dot(
                    ref[half, a * BS : (a + 1) * BS, :], right_ref[q], preferred_element_type=jnp.float32
                )

            return carry

        lax.fori_loop(0, ref.shape[0], one_half, 0)
        row += ref.shape[0]


def first_kernel(rights, *refs):
    right_refs, left_refs = refs[:rights], refs[rights:-6]
    acc_ref, right_all, right_tab, tab, table, sem = refs[-6:]
    row = 0
    for ref in right_refs:
        read_meta(ref, ref.shape[0], BS, tab, row)
        row += ref.shape[0]
    for ref in left_refs:
        read_meta(ref, ref.shape[0], 2 * BS, tab, row)
        row += ref.shape[0]
    copy = pltpu.make_async_copy(tab, table, sem)
    copy.start()
    acc_ref[...] = jnp.zeros_like(acc_ref)
    copy.wait()
    row = 0
    for ref in right_refs:
        for place in range(ref.shape[0]):
            q = table[row, 0]
            right_all[q] = ref[place, :BS, :]
            right_tab[0, q] = table[row, 1]
            right_tab[1, q] = table[row, 2]
            row += 1
    add_slots(left_refs, table, row, right_all, right_tab, acc_ref)


def last_kernel(acc_ref, right_all, right_tab, *refs):
    left_refs = refs[:-5]
    _, out_ref, tab, table, sem = refs[-5:]
    row = 0
    for ref in left_refs:
        read_meta(ref, ref.shape[0], 2 * BS, tab, row)
        row += ref.shape[0]
    copy = pltpu.make_async_copy(tab, table, sem)
    copy.start()
    copy.wait()
    add_slots(left_refs, table, 0, right_all, right_tab, acc_ref)
    out_ref[...] = acc_ref[:8].astype(jnp.bfloat16)


def table_scratch(panels):
    count = -(-sum(x.shape[0] for x in panels) // 8) * 8
    return [pltpu.VMEM((count, 128), jnp.int32), pltpu.SMEM((count, 128), jnp.int32), pltpu.SemaphoreType.DMA]


def first_product(lefts, rights):
    return pl.pallas_call(
        lambda *refs: first_kernel(len(rights), *refs),
        in_specs=[VMEM] * (len(lefts) + len(rights)),
        out_specs=(VMEM, VMEM, SMEM),
        out_shape=(
            pltpu.VMEM((9, BS, BS), jnp.float32),
            pltpu.VMEM((32, BS, BS), jnp.bfloat16),
            jax.ShapeDtypeStruct((2, 32), jnp.int32),
        ),
        scratch_shapes=table_scratch(rights + lefts),
        compiler_params=pltpu.CompilerParams(vmem_limit_bytes=GRANT),
    )(*near(rights + lefts))


def last_product(lefts, total, right_all, right_tab):
    return pl.pallas_call(
        last_kernel,
        in_specs=[VMEM, VMEM, SMEM] + [VMEM] * len(lefts),
        out_specs=(VMEM, VMEM),
        out_shape=(pltpu.VMEM((9, BS, BS), jnp.float32), jax.ShapeDtypeStruct((8, BS, BS), jnp.bfloat16)),
        input_output_aliases={0: 0},
        scratch_shapes=table_scratch(lefts),
        compiler_params=pltpu.CompilerParams(vmem_limit_bytes=GRANT),
    )(*near([total, right_all]), right_tab, *near(lefts))[1]


def panels(
    left_blocks,
    left_rows,
    left_cols,
    left_count,
    right_blocks,
    right_rows,
    right_cols,
    kept_rows,
    kept_cols,
):
    left_own, right_own = prepare(
        [
            left_blocks.reshape(2, 2 * BS, BS),
            right_blocks.reshape(BS, BS),
            left_rows.reshape(1, 4),
            left_cols.reshape(1, 4),
            kept_rows,
            kept_cols,
        ],
        [left_count, right_rows.reshape(1, 1), right_cols.reshape(1, 1)],
    )

    far = lax.ppermute(left_own, "x", mirror(2))
    across = lax.ppermute(left_own, "y", mirror(2))
    beside = lax.ppermute(left_own, "y", mirror(1))
    diagonal = lax.ppermute(across, "y", mirror(1))
    far_across = lax.ppermute(far, "y", mirror(2))
    far_beside = lax.ppermute(far, "y", mirror(1))
    far_diagonal = lax.ppermute(far_across, "y", mirror(1))
    early = [left_own, far, across, beside, diagonal, far_across, far_beside]
    late = [far_diagonal]
    for place, panel in enumerate([left_own, jnp.concatenate([beside, across]), diagonal]):
        got = [lax.ppermute(panel, "x", EVEN), lax.ppermute(panel, "x", ODD)]
        if place < 2:
            early += got
        else:
            late += got

    pair = jnp.stack([right_own, lax.ppermute(right_own, "h", SWAP)])
    four = jnp.concatenate([pair, lax.ppermute(pair, "c", SWAP)])
    one = lax.ppermute(four, ("z", "c"), along_z(1))
    two = lax.ppermute(four, ("z", "c"), along_z(2))
    three = lax.ppermute(two, ("z", "c"), along_z(1))
    opposite = lax.ppermute(two[:2], ("z", "c"), along_z(2))
    passed = jnp.concatenate([one, two, three, opposite])
    rights = [four, passed, lax.ppermute(passed, "c", SWAP)]

    carried = first_product(early, rights)
    return last_product(late, *carried).reshape(1, 1, 2, 4, BS, BS)


def solution(mesh):
    split = Mesh(mesh.devices.reshape(8, 2, 2, 4, 4), ROW + COL)
    return jax.shard_map(
        panels,
        mesh=split,
        in_specs=(
            P(ROW, COL, None, None, None),
            P(ROW, COL, None),
            P(ROW, COL, None),
            P(ROW, COL),
            P(ROW, COL, None, None, None),
            P(ROW, COL, None),
            P(ROW, COL, None),
            P(ROW, None),
            P(COL, None),
        ),
        out_specs=P(ROW, COL, None, None, None, None),
        check_vma=False,
    )
```

```python
import jax
import jax.numpy as jnp
from jax import lax
from jax.experimental import pallas as pl
from jax.experimental.pallas import tpu as pltpu
from jax.sharding import Mesh
from jax.sharding import PartitionSpec as P

RB = 16
BS = 256
META = 16
HALF = 2 * BS + META
RIGHT = BS + META
DEAD = 8
GRANT = 4 << 20
ROW = ("z", "h", "c")
COL = ("y", "x")
SWAP = [(0, 1), (1, 0)]


EVEN = [(0, 1), (1, 0), (2, 3), (3, 2)]
ODD = [(1, 2), (2, 1), (3, 0), (0, 3)]


VMEM = pl.BlockSpec(memory_space=pltpu.VMEM)
SMEM = pl.BlockSpec(memory_space=pltpu.SMEM)


def joined(first, second):
    first, second = (
        jnp.pad(panel, (place, (0, 0), (0, 0)), constant_values=-jnp.inf)
        for panel, place in ((first, (0, 2)), (second, (2, 0)))
    )
    return jnp.maximum(first, second)


def near(arrays):
    return [pltpu.with_memory_space_constraint(x, pltpu.VMEM) for x in arrays]


def along_z(step):
    up = [(2 * z, 2 * ((z + step) % 8)) for z in range(8)]
    return up + [(2 * z + 1, 2 * ((z - step) % 8) + 1) for z in range(8)]


def mirror(bit):
    return [(i, i ^ bit) for i in range(4)]


def write_meta(panel, values):
    lane = lax.broadcasted_iota(jnp.int32, (META, BS), 1)
    row = jnp.zeros((META, BS), jnp.int32)
    for place, value in enumerate(values):
        row = jnp.where(lane == place, value, row)
    panel[...] = row.astype(jnp.float32).astype(jnp.bfloat16)


def position(value, kept):
    place = jnp.int32(0)
    for n in range(1, kept.shape[1]):
        place = jnp.where(value == kept[0, n], n, place)
    return place


def prepare_kernel(*refs):
    blocks, right = refs[:2]
    count, right_row, right_col = refs[6:9]
    left_out, right_out = refs[9:11]
    rows, cols, kept_rows, kept_cols = refs[11:15]
    sems = refs[15]
    pairs = list(zip(refs[2:6], refs[11:15]))
    pairs += [(blocks.at[half], left_out.at[half, : 2 * BS]) for half in range(2)]
    pairs.append((right, right_out.at[:BS]))
    copies = [pltpu.make_async_copy(source, target, sems.at[n]) for n, (source, target) in enumerate(pairs)]
    for copy in copies:
        copy.start()
    panel_k = lax.axis_index("y") * 4 + lax.axis_index("x")
    own_q = lax.axis_index("z") * 4 + lax.axis_index("h") * 2 + lax.axis_index("c")
    for copy in copies[:4]:
        copy.wait()
    for half in range(2):
        values = []
        for slot in (2 * half, 2 * half + 1):
            col = cols[0, slot]
            code = (2 * panel_k + col // RB) * 2 + position(rows[0, slot], kept_rows)
            values += [jnp.where(slot < count[0, 0], code, -1), col % RB]
        write_meta(left_out.at[half, 2 * BS :], values)
    write_meta(right_out.at[BS:], [own_q, position(right_col[0, 0], kept_cols), right_row[0, 0]])
    for copy in copies[4:]:
        copy.wait()


def prepare(arrays, scalars):
    return pl.pallas_call(
        prepare_kernel,
        in_specs=[pl.BlockSpec(memory_space=pltpu.HBM)] * len(arrays) + [SMEM] * len(scalars),
        out_specs=(VMEM, VMEM),
        out_shape=(pltpu.VMEM((2, HALF, BS), jnp.bfloat16), pltpu.VMEM((RIGHT, BS), jnp.bfloat16)),
        scratch_shapes=[pltpu.SMEM(x.shape, jnp.int32) for x in arrays[2:]] + [pltpu.SemaphoreType.DMA((7,))],
        compiler_params=pltpu.CompilerParams(vmem_limit_bytes=GRANT),
    )(*[pltpu.with_memory_space_constraint(x, pltpu.HBM) for x in arrays], *scalars)


def read_meta(ref, count, first, tab, row):
    for place in range(count):
        tab[row + place, :] = ref[place, first : first + META, :128].astype(jnp.float32).astype(jnp.int32)[0]


def add_slots(left_refs, table, row, right_ref, right_tab, acc_ref):
    for ref in left_refs:

        def one_half(half, carry, ref=ref, row=row):
            for a in range(2):
                code = table[row + half, 2 * a]
                q = jnp.maximum(code, 0) // 2
                live = (code >= 0) & (table[row + half, 2 * a + 1] == right_tab[1, q])
                block = jnp.where(live, (code % 2) * 4 + right_tab[0, q], DEAD)
                acc_ref[block] += jnp.dot(
                    ref[half, a * BS : (a + 1) * BS, :], right_ref[q], preferred_element_type=jnp.float32
                )

            return carry

        lax.fori_loop(0, ref.shape[0], one_half, 0)
        row += ref.shape[0]


def first_kernel(rights, *refs):
    right_refs, left_refs = refs[:rights], refs[rights:-6]
    acc_ref, right_all, right_tab, tab, table, sem = refs[-6:]
    row = 0
    for ref in right_refs:
        read_meta(ref, ref.shape[0], BS, tab, row)
        row += ref.shape[0]
    for ref in left_refs:
        read_meta(ref, ref.shape[0], 2 * BS, tab, row)
        row += ref.shape[0]
    copy = pltpu.make_async_copy(tab, table, sem)
    copy.start()
    acc_ref[...] = jnp.zeros_like(acc_ref)
    copy.wait()
    row = 0
    for ref in right_refs:
        for place in range(ref.shape[0]):
            q = table[row, 0]
            right_all[q] = ref[place, :BS, :]
            right_tab[0, q] = table[row, 1]
            right_tab[1, q] = table[row, 2]
            row += 1
    add_slots(left_refs, table, row, right_all, right_tab, acc_ref)


def last_kernel(acc_ref, right_all, right_tab, *refs):
    left_refs = refs[:-5]
    _, out_ref, tab, table, sem = refs[-5:]
    row = 0
    for ref in left_refs:
        read_meta(ref, ref.shape[0], 2 * BS, tab, row)
        row += ref.shape[0]
    copy = pltpu.make_async_copy(tab, table, sem)
    copy.start()
    copy.wait()
    add_slots(left_refs, table, 0, right_all, right_tab, acc_ref)
    out_ref[...] = acc_ref[:8].astype(jnp.bfloat16)


def table_scratch(panels):
    count = -(-sum(x.shape[0] for x in panels) // 8) * 8
    return [pltpu.VMEM((count, 128), jnp.int32), pltpu.SMEM((count, 128), jnp.int32), pltpu.SemaphoreType.DMA]


def first_product(lefts, rights):
    return pl.pallas_call(
        lambda *refs: first_kernel(len(rights), *refs),
        in_specs=[VMEM] * (len(lefts) + len(rights)),
        out_specs=(VMEM, VMEM, SMEM),
        out_shape=(
            pltpu.VMEM((9, BS, BS), jnp.float32),
            pltpu.VMEM((32, BS, BS), jnp.bfloat16),
            jax.ShapeDtypeStruct((2, 32), jnp.int32),
        ),
        scratch_shapes=table_scratch(rights + lefts),
        compiler_params=pltpu.CompilerParams(vmem_limit_bytes=GRANT),
    )(*near(rights + lefts))


def last_product(lefts, total, right_all, right_tab):
    return pl.pallas_call(
        last_kernel,
        in_specs=[VMEM, VMEM, SMEM] + [VMEM] * len(lefts),
        out_specs=(VMEM, VMEM),
        out_shape=(pltpu.VMEM((9, BS, BS), jnp.float32), jax.ShapeDtypeStruct((8, BS, BS), jnp.bfloat16)),
        input_output_aliases={0: 0},
        scratch_shapes=table_scratch(lefts),
        compiler_params=pltpu.CompilerParams(vmem_limit_bytes=GRANT),
    )(*near([total, right_all]), right_tab, *near(lefts))[1]


def panels(
    left_blocks,
    left_rows,
    left_cols,
    left_count,
    right_blocks,
    right_rows,
    right_cols,
    kept_rows,
    kept_cols,
):
    left_own, right_own = prepare(
        [
            left_blocks.reshape(2, 2 * BS, BS),
            right_blocks.reshape(BS, BS),
            left_rows.reshape(1, 4),
            left_cols.reshape(1, 4),
            kept_rows,
            kept_cols,
        ],
        [left_count, right_rows.reshape(1, 1), right_cols.reshape(1, 1)],
    )

    far = lax.ppermute(left_own, "x", mirror(2))
    across = lax.ppermute(left_own, "y", mirror(2))
    beside = lax.ppermute(left_own, "y", mirror(1))
    diagonal = lax.ppermute(across, "y", mirror(1))
    far_across = lax.ppermute(far, "y", mirror(2))
    far_beside = lax.ppermute(far, "y", mirror(1))
    far_diagonal = lax.ppermute(far_across, "y", mirror(1))
    early = [left_own, far, across, beside, diagonal, far_across]
    late = [far_diagonal, far_beside]
    for place, panel in enumerate([left_own, joined(beside, across), diagonal]):
        got = [lax.ppermute(panel, "x", EVEN), lax.ppermute(panel, "x", ODD)]
        if place < 2:
            early += got
        else:
            late += got

    pair = jnp.stack([right_own, lax.ppermute(right_own, "h", SWAP)])
    four = jnp.concatenate([pair, lax.ppermute(pair, "c", SWAP)])
    one = lax.ppermute(four, ("z", "c"), along_z(1))
    two = lax.ppermute(four, ("z", "c"), along_z(2))
    three = lax.ppermute(two, ("z", "c"), along_z(1))
    opposite = lax.ppermute(two[:2], ("z", "c"), along_z(2))
    passed = jnp.concatenate([one, two, three, opposite])
    rights = [four, passed, lax.ppermute(passed, "c", SWAP)]

    carried = first_product(early, rights)
    return last_product(late, *carried).reshape(1, 1, 2, 4, BS, BS)


def solution(mesh):
    split = Mesh(mesh.devices.reshape(8, 2, 2, 4, 4), ROW + COL)
    return jax.shard_map(
        panels,
        mesh=split,
        in_specs=(
            P(ROW, COL, None, None, None),
            P(ROW, COL, None),
            P(ROW, COL, None),
            P(ROW, COL),
            P(ROW, COL, None, None, None),
            P(ROW, COL, None),
            P(ROW, COL, None),
            P(ROW, None),
            P(COL, None),
        ),
        out_specs=P(ROW, COL, None, None, None, None),
        check_vma=False,
    )
```

```python
import jax
import jax.numpy as jnp
from jax import lax
from jax.experimental import pallas as pl
from jax.experimental.pallas import tpu as pltpu
from jax.sharding import Mesh
from jax.sharding import PartitionSpec as P

RB = 16
BS = 256
META = 16
HALF = 2 * BS + META
RIGHT = BS + META
DEAD = 8
GRANT = 4 << 20
ROW = ("z", "h", "c")
COL = ("y", "x")
SWAP = [(0, 1), (1, 0)]


EVEN = [(0, 1), (1, 0), (2, 3), (3, 2)]
ODD = [(1, 2), (2, 1), (3, 0), (0, 3)]


VMEM = pl.BlockSpec(memory_space=pltpu.VMEM)
SMEM = pl.BlockSpec(memory_space=pltpu.SMEM)


def joined(first, second):
    first, second = (
        jnp.pad(panel, (place, (0, 0), (0, 0)), constant_values=-jnp.inf)
        for panel, place in ((first, (0, 2)), (second, (2, 0)))
    )
    return jnp.maximum(first, second)


def near(arrays):
    return [pltpu.with_memory_space_constraint(x, pltpu.VMEM) for x in arrays]


def along_z(step):
    up = [(2 * z, 2 * ((z + step) % 8)) for z in range(8)]
    return up + [(2 * z + 1, 2 * ((z - step) % 8) + 1) for z in range(8)]


def mirror(bit):
    return [(i, i ^ bit) for i in range(4)]


def write_meta(panel, values):
    lane = lax.broadcasted_iota(jnp.int32, (META, BS), 1)
    row = jnp.zeros((META, BS), jnp.int32)
    for place, value in enumerate(values):
        row = jnp.where(lane == place, value, row)
    panel[...] = row.astype(jnp.float32).astype(jnp.bfloat16)


def position(value, kept):
    place = jnp.int32(0)
    for n in range(1, kept.shape[1]):
        place = jnp.where(value == kept[0, n], n, place)
    return place


def prepare_kernel(*refs):
    blocks, right = refs[:2]
    count, right_row, right_col = refs[6:9]
    left_out, right_out = refs[9:11]
    rows, cols, kept_rows, kept_cols = refs[11:15]
    sems = refs[15]
    pairs = list(zip(refs[2:6], refs[11:15]))
    pairs += [(blocks.at[half], left_out.at[half, : 2 * BS]) for half in range(2)]
    pairs.append((right, right_out.at[:BS]))
    copies = [pltpu.make_async_copy(source, target, sems.at[n]) for n, (source, target) in enumerate(pairs)]
    for copy in copies:
        copy.start()
    panel_k = lax.axis_index("y") * 4 + lax.axis_index("x")
    own_q = lax.axis_index("z") * 4 + lax.axis_index("h") * 2 + lax.axis_index("c")
    for copy in copies[:4]:
        copy.wait()
    for half in range(2):
        values = []
        for slot in (2 * half, 2 * half + 1):
            col = cols[0, slot]
            code = (2 * panel_k + col // RB) * 2 + position(rows[0, slot], kept_rows)
            values += [jnp.where(slot < count[0, 0], code, -1), col % RB]
        write_meta(left_out.at[half, 2 * BS :], values)
    write_meta(right_out.at[BS:], [own_q, position(right_col[0, 0], kept_cols), right_row[0, 0]])
    for copy in copies[4:]:
        copy.wait()


def prepare(arrays, scalars):
    return pl.pallas_call(
        prepare_kernel,
        in_specs=[pl.BlockSpec(memory_space=pltpu.HBM)] * len(arrays) + [SMEM] * len(scalars),
        out_specs=(VMEM, VMEM),
        out_shape=(pltpu.VMEM((2, HALF, BS), jnp.bfloat16), pltpu.VMEM((RIGHT, BS), jnp.bfloat16)),
        scratch_shapes=[pltpu.SMEM(x.shape, jnp.int32) for x in arrays[2:]] + [pltpu.SemaphoreType.DMA((7,))],
        compiler_params=pltpu.CompilerParams(vmem_limit_bytes=GRANT),
    )(*[pltpu.with_memory_space_constraint(x, pltpu.HBM) for x in arrays], *scalars)


def read_meta(ref, count, first, tab, row):
    for place in range(count):
        tab[row + place, :] = ref[place, first : first + META, :128].astype(jnp.float32).astype(jnp.int32)[0]


def add_slots(left_refs, table, row, right_ref, right_tab, acc_ref):
    for ref in left_refs:

        def one_half(half, carry, ref=ref, row=row):
            for a in range(2):
                code = table[row + half, 2 * a]
                q = jnp.maximum(code, 0) // 2
                live = (code >= 0) & (table[row + half, 2 * a + 1] == right_tab[1, q])
                block = jnp.where(live, (code % 2) * 4 + right_tab[0, q], DEAD)
                acc_ref[block] += jnp.dot(
                    ref[half, a * BS : (a + 1) * BS, :], right_ref[q], preferred_element_type=jnp.float32
                )

            return carry

        lax.fori_loop(0, ref.shape[0], one_half, 0)
        row += ref.shape[0]


def first_kernel(rights, *refs):
    right_refs, left_refs = refs[:rights], refs[rights:-7]
    acc_ref, right_all, kept_tab, tab, table, sem, right_tab = refs[-7:]
    row = 0
    for ref in right_refs:
        read_meta(ref, ref.shape[0], BS, tab, row)
        row += ref.shape[0]
    for ref in left_refs:
        read_meta(ref, ref.shape[0], 2 * BS, tab, row)
        row += ref.shape[0]
    copy = pltpu.make_async_copy(tab, table, sem)
    copy.start()
    acc_ref[...] = jnp.zeros_like(acc_ref)
    kept_tab[...] = tab[:32, :]
    copy.wait()
    row = 0
    for ref in right_refs:
        for place in range(ref.shape[0]):
            right_all[table[row, 0]] = ref[place, :BS, :]
            row += 1
    look_up(table, right_tab)
    add_slots(left_refs, table, 32, right_all, right_tab, acc_ref)


def look_up(table, right_tab):
    for row in range(32):
        q = table[row, 0]
        right_tab[0, q] = table[row, 1]
        right_tab[1, q] = table[row, 2]


def last_kernel(acc_ref, right_all, kept_tab, *refs):
    left_refs = refs[:-6]
    _, out_ref, tab, table, sem, right_tab = refs[-6:]
    tab[:32, :] = kept_tab[...]
    row = 32
    for ref in left_refs:
        read_meta(ref, ref.shape[0], 2 * BS, tab, row)
        row += ref.shape[0]
    copy = pltpu.make_async_copy(tab, table, sem)
    copy.start()
    copy.wait()
    look_up(table, right_tab)
    add_slots(left_refs, table, 32, right_all, right_tab, acc_ref)
    out_ref[...] = acc_ref[:8].astype(jnp.bfloat16)


def table_scratch(panels):
    count = 32 + -(-sum(x.shape[0] for x in panels) // 8) * 8
    return [
        pltpu.VMEM((count, 128), jnp.int32),
        pltpu.SMEM((count, 128), jnp.int32),
        pltpu.SemaphoreType.DMA,
        pltpu.SMEM((2, 32), jnp.int32),
    ]


def first_product(lefts, rights):
    return pl.pallas_call(
        lambda *refs: first_kernel(len(rights), *refs),
        in_specs=[VMEM] * (len(lefts) + len(rights)),
        out_specs=(VMEM, VMEM, VMEM),
        out_shape=(
            pltpu.VMEM((9, BS, BS), jnp.float32),
            pltpu.VMEM((32, BS, BS), jnp.bfloat16),
            pltpu.VMEM((32, 128), jnp.int32),
        ),
        scratch_shapes=table_scratch(lefts),
        compiler_params=pltpu.CompilerParams(vmem_limit_bytes=GRANT),
    )(*near(rights + lefts))


def last_product(lefts, *carried):
    return pl.pallas_call(
        last_kernel,
        in_specs=[VMEM] * (len(carried) + len(lefts)),
        out_specs=(VMEM, VMEM),
        out_shape=(pltpu.VMEM((9, BS, BS), jnp.float32), jax.ShapeDtypeStruct((8, BS, BS), jnp.bfloat16)),
        input_output_aliases={0: 0},
        scratch_shapes=table_scratch(lefts),
        compiler_params=pltpu.CompilerParams(vmem_limit_bytes=GRANT),
    )(*near(list(carried) + lefts))[1]


def panels(
    left_blocks,
    left_rows,
    left_cols,
    left_count,
    right_blocks,
    right_rows,
    right_cols,
    kept_rows,
    kept_cols,
):
    left_own, right_own = prepare(
        [
            left_blocks.reshape(2, 2 * BS, BS),
            right_blocks.reshape(BS, BS),
            left_rows.reshape(1, 4),
            left_cols.reshape(1, 4),
            kept_rows,
            kept_cols,
        ],
        [left_count, right_rows.reshape(1, 1), right_cols.reshape(1, 1)],
    )

    far = lax.ppermute(left_own, "x", mirror(2))
    across = lax.ppermute(left_own, "y", mirror(2))
    beside = lax.ppermute(left_own, "y", mirror(1))
    diagonal = lax.ppermute(across, "y", mirror(1))
    far_across = lax.ppermute(far, "y", mirror(2))
    far_beside = lax.ppermute(far, "y", mirror(1))
    far_diagonal = lax.ppermute(far_across, "y", mirror(1))
    early = [left_own, far, across, beside, diagonal, far_across]
    late = [far_diagonal, far_beside]
    for place, panel in enumerate([left_own, joined(beside, across), diagonal]):
        got = [lax.ppermute(panel, "x", EVEN), lax.ppermute(panel, "x", ODD)]
        if place < 2:
            early += got
        else:
            late += got

    pair = jnp.stack([right_own, lax.ppermute(right_own, "h", SWAP)])
    four = jnp.concatenate([pair, lax.ppermute(pair, "c", SWAP)])
    one = lax.ppermute(four, ("z", "c"), along_z(1))
    two = lax.ppermute(four, ("z", "c"), along_z(2))
    three = lax.ppermute(two, ("z", "c"), along_z(1))
    opposite = lax.ppermute(two[:2], ("z", "c"), along_z(2))
    passed = jnp.concatenate([one, two, three, opposite])
    rights = [four, passed, lax.ppermute(passed, "c", SWAP)]

    carried = first_product(early, rights)
    return last_product(late, *carried).reshape(1, 1, 2, 4, BS, BS)


def solution(mesh):
    split = Mesh(mesh.devices.reshape(8, 2, 2, 4, 4), ROW + COL)
    return jax.shard_map(
        panels,
        mesh=split,
        in_specs=(
            P(ROW, COL, None, None, None),
            P(ROW, COL, None),
            P(ROW, COL, None),
            P(ROW, COL),
            P(ROW, COL, None, None, None),
            P(ROW, COL, None),
            P(ROW, COL, None),
            P(ROW, None),
            P(COL, None),
        ),
        out_specs=P(ROW, COL, None, None, None, None),
        check_vma=False,
    )
```

```python
import jax
import jax.numpy as jnp
from jax import lax
from jax.experimental import pallas as pl
from jax.experimental.pallas import tpu as pltpu
from jax.sharding import Mesh
from jax.sharding import PartitionSpec as P

RB = 16
BS = 256
META = 16
HALF = 2 * BS + META
RIGHT = BS + META
DEAD = 8
GRANT = 4 << 20
ROW = ("z", "h", "c")
COL = ("y", "x")
SWAP = [(0, 1), (1, 0)]


EVEN = [(0, 1), (1, 0), (2, 3), (3, 2)]
ODD = [(1, 2), (2, 1), (3, 0), (0, 3)]


VMEM = pl.BlockSpec(memory_space=pltpu.VMEM)
SMEM = pl.BlockSpec(memory_space=pltpu.SMEM)


def joined(first, second):
    first, second = (
        jnp.pad(panel, (place, (0, 0), (0, 0)), constant_values=-jnp.inf)
        for panel, place in ((first, (0, 2)), (second, (2, 0)))
    )
    return jnp.maximum(first, second)


def near(arrays):
    return [pltpu.with_memory_space_constraint(x, pltpu.VMEM) for x in arrays]


def along_z(step):
    up = [(2 * z, 2 * ((z + step) % 8)) for z in range(8)]
    return up + [(2 * z + 1, 2 * ((z - step) % 8) + 1) for z in range(8)]


def mirror(bit):
    return [(i, i ^ bit) for i in range(4)]


def write_meta(panel, values):
    lane = lax.broadcasted_iota(jnp.int32, (META, BS), 1)
    row = jnp.zeros((META, BS), jnp.int32)
    for place, value in enumerate(values):
        row = jnp.where(lane == place, value, row)
    panel[...] = row.astype(jnp.float32).astype(jnp.bfloat16)


def position(value, kept):
    place = jnp.int32(0)
    for n in range(1, kept.shape[1]):
        place = jnp.where(value == kept[0, n], n, place)
    return place


def prepare_kernel(*refs):
    blocks, right = refs[:2]
    count, right_row, right_col = refs[6:9]
    left_out, right_out = refs[9:11]
    rows, cols, kept_rows, kept_cols = refs[11:15]
    sems = refs[15]
    pairs = list(zip(refs[2:6], refs[11:15]))
    pairs += [(blocks.at[half], left_out.at[half, : 2 * BS]) for half in range(2)]
    pairs.append((right, right_out.at[:BS]))
    copies = [pltpu.make_async_copy(source, target, sems.at[n]) for n, (source, target) in enumerate(pairs)]
    for copy in copies:
        copy.start()
    panel_k = lax.axis_index("y") * 4 + lax.axis_index("x")
    own_q = lax.axis_index("z") * 4 + lax.axis_index("h") * 2 + lax.axis_index("c")
    for copy in copies[:4]:
        copy.wait()
    for half in range(2):
        values = []
        for slot in (2 * half, 2 * half + 1):
            col = cols[0, slot]
            code = (2 * panel_k + col // RB) * 2 + position(rows[0, slot], kept_rows)
            values += [jnp.where(slot < count[0, 0], code, -1), col % RB]
        write_meta(left_out.at[half, 2 * BS :], values)
    write_meta(right_out.at[BS:], [own_q, position(right_col[0, 0], kept_cols), right_row[0, 0]])
    for copy in copies[4:]:
        copy.wait()


def prepare(arrays, scalars):
    return pl.pallas_call(
        prepare_kernel,
        in_specs=[pl.BlockSpec(memory_space=pltpu.HBM)] * len(arrays) + [SMEM] * len(scalars),
        out_specs=(VMEM, VMEM),
        out_shape=(pltpu.VMEM((2, HALF, BS), jnp.bfloat16), pltpu.VMEM((RIGHT, BS), jnp.bfloat16)),
        scratch_shapes=[pltpu.SMEM(x.shape, jnp.int32) for x in arrays[2:]] + [pltpu.SemaphoreType.DMA((7,))],
        compiler_params=pltpu.CompilerParams(vmem_limit_bytes=GRANT),
    )(*[pltpu.with_memory_space_constraint(x, pltpu.HBM) for x in arrays], *scalars)


def read_meta(ref, count, first, tab, row):
    for place in range(count):
        tab[row + place, :] = ref[place, first : first + META, :128].astype(jnp.float32).astype(jnp.int32)[0]


def add_slots(left_refs, table, row, right_ref, right_tab, acc_ref):
    for ref in left_refs:

        def one_half(half, carry, ref=ref, row=row):
            for a in range(2):
                code = table[row + half, 2 * a]
                q = jnp.maximum(code, 0) // 2
                live = (code >= 0) & (table[row + half, 2 * a + 1] == right_tab[1, q])
                block = jnp.where(live, (code % 2) * 4 + right_tab[0, q], DEAD)
                acc_ref[block] += jnp.dot(
                    ref[half, a * BS : (a + 1) * BS, :], right_ref[right_tab[2, q]], preferred_element_type=jnp.float32
                )

            return carry

        lax.fori_loop(0, ref.shape[0], one_half, 0)
        row += ref.shape[0]


def first_kernel(rights, *refs):
    right_refs, left_refs = refs[:rights], refs[rights:-7]
    acc_ref, right_all, kept_tab, tab, table, sem, right_tab = refs[-7:]
    row = 0
    for ref in right_refs:
        read_meta(ref, ref.shape[0], BS, tab, row)
        row += ref.shape[0]
    for ref in left_refs:
        read_meta(ref, ref.shape[0], 2 * BS, tab, row)
        row += ref.shape[0]
    copy = pltpu.make_async_copy(tab, table, sem)
    copy.start()
    acc_ref[...] = jnp.zeros_like(acc_ref)
    kept_tab[...] = tab[:32, :]
    row = 0
    for ref in right_refs:
        right_all[row : row + ref.shape[0]] = ref[:, :BS, :]
        row += ref.shape[0]
    copy.wait()
    look_up(table, right_tab)
    add_slots(left_refs, table, 32, right_all, right_tab, acc_ref)


def look_up(table, right_tab):
    for row in range(32):
        q = table[row, 0]
        right_tab[0, q] = table[row, 1]
        right_tab[1, q] = table[row, 2]
        right_tab[2, q] = row


def last_kernel(acc_ref, right_all, kept_tab, *refs):
    left_refs = refs[:-6]
    _, out_ref, tab, table, sem, right_tab = refs[-6:]
    tab[:32, :] = kept_tab[...]
    row = 32
    for ref in left_refs:
        read_meta(ref, ref.shape[0], 2 * BS, tab, row)
        row += ref.shape[0]
    copy = pltpu.make_async_copy(tab, table, sem)
    copy.start()
    copy.wait()
    look_up(table, right_tab)
    add_slots(left_refs, table, 32, right_all, right_tab, acc_ref)
    out_ref[...] = acc_ref[:8].astype(jnp.bfloat16)


def table_scratch(panels):
    count = 32 + -(-sum(x.shape[0] for x in panels) // 8) * 8
    return [
        pltpu.VMEM((count, 128), jnp.int32),
        pltpu.SMEM((count, 128), jnp.int32),
        pltpu.SemaphoreType.DMA,
        pltpu.SMEM((3, 32), jnp.int32),
    ]


def first_product(lefts, rights):
    return pl.pallas_call(
        lambda *refs: first_kernel(len(rights), *refs),
        in_specs=[VMEM] * (len(lefts) + len(rights)),
        out_specs=(VMEM, VMEM, VMEM),
        out_shape=(
            pltpu.VMEM((9, BS, BS), jnp.float32),
            pltpu.VMEM((32, BS, BS), jnp.bfloat16),
            pltpu.VMEM((32, 128), jnp.int32),
        ),
        scratch_shapes=table_scratch(lefts),
        compiler_params=pltpu.CompilerParams(vmem_limit_bytes=GRANT),
    )(*near(rights + lefts))


def last_product(lefts, *carried):
    return pl.pallas_call(
        last_kernel,
        in_specs=[VMEM] * (len(carried) + len(lefts)),
        out_specs=(VMEM, VMEM),
        out_shape=(pltpu.VMEM((9, BS, BS), jnp.float32), jax.ShapeDtypeStruct((8, BS, BS), jnp.bfloat16)),
        input_output_aliases={0: 0},
        scratch_shapes=table_scratch(lefts),
        compiler_params=pltpu.CompilerParams(vmem_limit_bytes=GRANT),
    )(*near(list(carried) + lefts))[1]


def panels(
    left_blocks,
    left_rows,
    left_cols,
    left_count,
    right_blocks,
    right_rows,
    right_cols,
    kept_rows,
    kept_cols,
):
    left_own, right_own = prepare(
        [
            left_blocks.reshape(2, 2 * BS, BS),
            right_blocks.reshape(BS, BS),
            left_rows.reshape(1, 4),
            left_cols.reshape(1, 4),
            kept_rows,
            kept_cols,
        ],
        [left_count, right_rows.reshape(1, 1), right_cols.reshape(1, 1)],
    )

    far = lax.ppermute(left_own, "x", mirror(2))
    across = lax.ppermute(left_own, "y", mirror(2))
    beside = lax.ppermute(left_own, "y", mirror(1))
    diagonal = lax.ppermute(across, "y", mirror(1))
    far_across = lax.ppermute(far, "y", mirror(2))
    far_beside = lax.ppermute(far, "y", mirror(1))
    far_diagonal = lax.ppermute(far_across, "y", mirror(1))
    early = [left_own, far, across, beside, diagonal, far_across, far_beside]
    late = [far_diagonal]
    for place, panel in enumerate([left_own, joined(beside, across), diagonal]):
        got = [lax.ppermute(panel, "x", EVEN), lax.ppermute(panel, "x", ODD)]
        if place < 2:
            early += got
        else:
            late += got

    pair = jnp.stack([right_own, lax.ppermute(right_own, "h", SWAP)])
    four = jnp.concatenate([pair, lax.ppermute(pair, "c", SWAP)])
    one = lax.ppermute(four, ("z", "c"), along_z(1))
    two = lax.ppermute(four, ("z", "c"), along_z(2))
    three = lax.ppermute(two, ("z", "c"), along_z(1))
    opposite = lax.ppermute(two[:2], ("z", "c"), along_z(2))
    passed = jnp.concatenate([one, two, three, opposite])
    rights = [four, passed, lax.ppermute(passed, "c", SWAP)]

    carried = first_product(early, rights)
    return last_product(late, *carried).reshape(1, 1, 2, 4, BS, BS)


def solution(mesh):
    split = Mesh(mesh.devices.reshape(8, 2, 2, 4, 4), ROW + COL)
    return jax.shard_map(
        panels,
        mesh=split,
        in_specs=(
            P(ROW, COL, None, None, None),
            P(ROW, COL, None),
            P(ROW, COL, None),
            P(ROW, COL),
            P(ROW, COL, None, None, None),
            P(ROW, COL, None),
            P(ROW, COL, None),
            P(ROW, None),
            P(COL, None),
        ),
        out_specs=P(ROW, COL, None, None, None, None),
        check_vma=False,
    )
```

```python
import jax
import jax.numpy as jnp
from jax import lax
from jax.experimental import pallas as pl
from jax.experimental.pallas import tpu as pltpu
from jax.sharding import Mesh
from jax.sharding import PartitionSpec as P

RB = 16
BS = 256
META = 16
HALF = 2 * BS + META
RIGHT = BS + META
DEAD = 8
GRANT = 4 << 20
ROW = ("z", "h", "c")
COL = ("y", "x")
SWAP = [(0, 1), (1, 0)]


EVEN = [(0, 1), (1, 0), (2, 3), (3, 2)]
ODD = [(1, 2), (2, 1), (3, 0), (0, 3)]


VMEM = pl.BlockSpec(memory_space=pltpu.VMEM)
SMEM = pl.BlockSpec(memory_space=pltpu.SMEM)


def joined(first, second):
    first, second = (
        jnp.pad(panel, (place, (0, 0), (0, 0)), constant_values=-jnp.inf)
        for panel, place in ((first, (0, 2)), (second, (2, 0)))
    )
    return jnp.maximum(first, second)


def near(arrays):
    return [pltpu.with_memory_space_constraint(x, pltpu.VMEM) for x in arrays]


def along_z(step):
    up = [(2 * z, 2 * ((z + step) % 8)) for z in range(8)]
    return up + [(2 * z + 1, 2 * ((z - step) % 8) + 1) for z in range(8)]


def mirror(bit):
    return [(i, i ^ bit) for i in range(4)]


def write_meta(panel, values):
    lane = lax.broadcasted_iota(jnp.int32, (META, BS), 1)
    row = jnp.zeros((META, BS), jnp.int32)
    for place, value in enumerate(values):
        row = jnp.where(lane == place, value, row)
    panel[...] = row.astype(jnp.float32).astype(jnp.bfloat16)


def position(value, kept):
    place = jnp.int32(0)
    for n in range(1, kept.shape[1]):
        place = jnp.where(value == kept[0, n], n, place)
    return place


def prepare_kernel(*refs):
    blocks, right = refs[:2]
    count, right_row, right_col = refs[6:9]
    left_out, right_out = refs[9:11]
    rows, cols, kept_rows, kept_cols = refs[11:15]
    sems = refs[15]
    pairs = list(zip(refs[2:6], refs[11:15]))
    pairs += [(blocks.at[half], left_out.at[half, : 2 * BS]) for half in range(2)]
    pairs.append((right, right_out.at[:BS]))
    copies = [pltpu.make_async_copy(source, target, sems.at[n]) for n, (source, target) in enumerate(pairs)]
    for copy in copies:
        copy.start()
    panel_k = lax.axis_index("y") * 4 + lax.axis_index("x")
    own_q = lax.axis_index("z") * 4 + lax.axis_index("h") * 2 + lax.axis_index("c")
    for copy in copies[:4]:
        copy.wait()
    for half in range(2):
        values = []
        for slot in (2 * half, 2 * half + 1):
            col = cols[0, slot]
            code = (2 * panel_k + col // RB) * 2 + position(rows[0, slot], kept_rows)
            values += [jnp.where(slot < count[0, 0], code, -1), col % RB]
        write_meta(left_out.at[half, 2 * BS :], values)
    write_meta(right_out.at[BS:], [own_q, position(right_col[0, 0], kept_cols), right_row[0, 0]])
    for copy in copies[4:]:
        copy.wait()


def prepare(arrays, scalars):
    return pl.pallas_call(
        prepare_kernel,
        in_specs=[pl.BlockSpec(memory_space=pltpu.HBM)] * len(arrays) + [SMEM] * len(scalars),
        out_specs=(VMEM, VMEM),
        out_shape=(pltpu.VMEM((2, HALF, BS), jnp.bfloat16), pltpu.VMEM((RIGHT, BS), jnp.bfloat16)),
        scratch_shapes=[pltpu.SMEM(x.shape, jnp.int32) for x in arrays[2:]] + [pltpu.SemaphoreType.DMA((7,))],
        compiler_params=pltpu.CompilerParams(vmem_limit_bytes=GRANT),
    )(*[pltpu.with_memory_space_constraint(x, pltpu.HBM) for x in arrays], *scalars)


def read_meta(ref, count, first, tab, row):
    for place in range(count):
        tab[row + place, :] = ref[place, first : first + META, :128].astype(jnp.float32).astype(jnp.int32)[0]


def add_slots(left_refs, table, row, right_ref, right_tab, acc_ref):
    for ref in left_refs:

        def one_half(half, carry, ref=ref, row=row):
            for a in range(2):
                code = table[row + half, 2 * a]
                q = jnp.maximum(code, 0) // 2
                live = (code >= 0) & (table[row + half, 2 * a + 1] == right_tab[1, q])
                block = jnp.where(live, (code % 2) * 4 + right_tab[0, q], DEAD)
                acc_ref[block] += jnp.dot(
                    ref[half, a * BS : (a + 1) * BS, :], right_ref[right_tab[2, q]], preferred_element_type=jnp.float32
                )

            return carry

        lax.fori_loop(0, ref.shape[0], one_half, 0)
        row += ref.shape[0]


def first_kernel(rights, *refs):
    right_refs, left_refs = refs[:rights], refs[rights:-7]
    acc_ref, right_all, kept_tab, tab, table, sem, right_tab = refs[-7:]
    row = 0
    for ref in right_refs:
        read_meta(ref, ref.shape[0], BS, tab, row)
        row += ref.shape[0]
    for ref in left_refs:
        read_meta(ref, ref.shape[0], 2 * BS, tab, row)
        row += ref.shape[0]
    copy = pltpu.make_async_copy(tab, table, sem)
    copy.start()
    acc_ref[...] = jnp.zeros_like(acc_ref)
    kept_tab[...] = tab[:32, :]
    row = 0
    for ref in right_refs:
        right_all[row : row + ref.shape[0]] = ref[:, :BS, :]
        row += ref.shape[0]
    copy.wait()
    look_up(table, right_tab)
    add_slots(left_refs, table, 32, right_all, right_tab, acc_ref)


def look_up(table, right_tab):
    for row in range(32):
        q = table[row, 0]
        right_tab[0, q] = table[row, 1]
        right_tab[1, q] = table[row, 2]
        right_tab[2, q] = row


def last_kernel(acc_ref, right_all, kept_tab, *refs):
    left_refs = refs[:-6]
    _, out_ref, tab, table, sem, right_tab = refs[-6:]
    tab[:32, :] = kept_tab[...]
    row = 32
    for ref in left_refs:
        read_meta(ref, ref.shape[0], 2 * BS, tab, row)
        row += ref.shape[0]
    copy = pltpu.make_async_copy(tab, table, sem)
    copy.start()
    copy.wait()
    look_up(table, right_tab)
    add_slots(left_refs, table, 32, right_all, right_tab, acc_ref)
    out_ref[...] = acc_ref[:8].astype(jnp.bfloat16)


def table_scratch(panels):
    count = 32 + -(-sum(x.shape[0] for x in panels) // 8) * 8
    return [
        pltpu.VMEM((count, 128), jnp.int32),
        pltpu.SMEM((count, 128), jnp.int32),
        pltpu.SemaphoreType.DMA,
        pltpu.SMEM((3, 32), jnp.int32),
    ]


def first_product(lefts, rights):
    return pl.pallas_call(
        lambda *refs: first_kernel(len(rights), *refs),
        in_specs=[VMEM] * (len(lefts) + len(rights)),
        out_specs=(VMEM, VMEM, VMEM),
        out_shape=(
            pltpu.VMEM((9, BS, BS), jnp.float32),
            pltpu.VMEM((32, BS, BS), jnp.bfloat16),
            pltpu.VMEM((32, 128), jnp.int32),
        ),
        scratch_shapes=table_scratch(lefts),
        compiler_params=pltpu.CompilerParams(vmem_limit_bytes=GRANT),
    )(*near(rights + lefts))


def last_product(lefts, *carried):
    return pl.pallas_call(
        last_kernel,
        in_specs=[VMEM] * (len(carried) + len(lefts)),
        out_specs=(VMEM, VMEM),
        out_shape=(pltpu.VMEM((9, BS, BS), jnp.float32), jax.ShapeDtypeStruct((8, BS, BS), jnp.bfloat16)),
        input_output_aliases={0: 0},
        scratch_shapes=table_scratch(lefts),
        compiler_params=pltpu.CompilerParams(vmem_limit_bytes=GRANT),
    )(*near(list(carried) + lefts))[1]


def panels(
    left_blocks,
    left_rows,
    left_cols,
    left_count,
    right_blocks,
    right_rows,
    right_cols,
    kept_rows,
    kept_cols,
):
    left_own, right_own = prepare(
        [
            left_blocks.reshape(2, 2 * BS, BS),
            right_blocks.reshape(BS, BS),
            left_rows.reshape(1, 4),
            left_cols.reshape(1, 4),
            kept_rows,
            kept_cols,
        ],
        [left_count, right_rows.reshape(1, 1), right_cols.reshape(1, 1)],
    )

    far = lax.ppermute(left_own, "x", mirror(2))
    across = lax.ppermute(left_own, "y", mirror(2))
    beside = lax.ppermute(left_own, "y", mirror(1))
    diagonal = lax.ppermute(across, "y", mirror(1))
    far_across = lax.ppermute(far, "y", mirror(2))
    far_beside = lax.ppermute(far, "y", mirror(1))
    far_diagonal = lax.ppermute(far_across, "y", mirror(1))
    early = [left_own, far, across, beside, diagonal, far_across, far_beside]
    late = [far_diagonal]
    for place, panel in enumerate([left_own, joined(beside, across), diagonal]):
        got = [lax.ppermute(panel, "x", EVEN), lax.ppermute(panel, "x", ODD)]
        if place < 2:
            early += got
        else:
            late += got

    pair = jnp.stack([right_own, lax.ppermute(right_own, "h", SWAP)])
    four = jnp.concatenate([pair, lax.ppermute(pair, "c", SWAP)])
    one = lax.ppermute(four, ("z", "c"), along_z(1))
    two = lax.ppermute(four, ("z", "c"), along_z(2))
    three = lax.ppermute(two, ("z", "c"), along_z(1))
    opposite = lax.ppermute(two[:2], ("z", "c"), along_z(2))
    near_two = jnp.concatenate([one, two])
    far_two = jnp.concatenate([three, opposite])
    rights = [four, near_two, lax.ppermute(near_two, "c", SWAP), far_two, lax.ppermute(far_two, "c", SWAP)]

    carried = first_product(early, rights)
    return last_product(late, *carried).reshape(1, 1, 2, 4, BS, BS)


def solution(mesh):
    split = Mesh(mesh.devices.reshape(8, 2, 2, 4, 4), ROW + COL)
    return jax.shard_map(
        panels,
        mesh=split,
        in_specs=(
            P(ROW, COL, None, None, None),
            P(ROW, COL, None),
            P(ROW, COL, None),
            P(ROW, COL),
            P(ROW, COL, None, None, None),
            P(ROW, COL, None),
            P(ROW, COL, None),
            P(ROW, None),
            P(COL, None),
        ),
        out_specs=P(ROW, COL, None, None, None, None),
        check_vma=False,
    )
```
